32 devices in a mesh: sec: 4 (over y, x), pair: 8 (over z, core).
Axes of the slice: x: 2, y: 2, z: 4, core: 2. Of those that a mesh axis runs over, the one named last changes fastest.
Arguments:
- left_ops: bfloat16 [4, 528, 256, 256], P('sec', 'pair'), may hold values from -6 to 6
- rotation: bfloat16 [4, 256, 128], P('sec'), may hold values from -0.375 to 0.375
- integrals: bfloat16 [528, 528], replicated, may hold values from -0.25 to 0.25
- right_ops: bfloat16 [4, 528, 128, 128], P('sec', 'pair'), may hold values from -0.001953125 to 0.001953125
- states: bfloat16 [4, 16, 128, 128], P('sec', None, 'pair'), may hold values from -6 to 6
- sector_sizes: int32 [4], P('sec'), may hold values from 32 to 128, as said below
- couplings: int32 [4, 4], P('sec'), may hold values from -1 to 3, as said below
- pair_order: int32 [528], replicated, may hold values from 0 to 527, each once
Outputs:
- sigma: float32 [4, 16, 128, 128], P('sec', None, 'pair')
The draws below stay inside these ranges and needn't reach their ends.
Inputs may be any that keep to these rules, and one draw needn't show every extreme that they name: `sector_sizes`: some sector keeps all 128 states and some keeps 128 // 4. `couplings`: each row lists 1 to 4 distinct sectors in its first slots and -1 in the rest; some row is full and some lists one sector. `pair_order`: each pair appears once.
All inputs are finite; a program needn't handle non-finite values.
Results may differ from the reference program's by a relative error of at most 0.0064.
Values may be sent and summed in bfloat16 or wider, within the bound.
A program may use at most 64 MiB of HBM per device.

```python
import jax
import jax.numpy as jnp
from jax import lax

B0 = 256
M = 128
MR = 128
P_SIZE = 528
ROOTS = 16
KMAX = 4
SECTORS = 4


def draw_sector_sizes(key, part):
    base = jax.random.fold_in(key, 11)
    first, second, third = jax.random.split(base, 3)
    sizes = jax.random.randint(first, (SECTORS,), M // 4, M + 1)
    top = jax.random.randint(second, (), 0, SECTORS)
    offset = jax.random.randint(third, (), 1, SECTORS)
    bottom = (top + offset) % SECTORS
    index = jnp.arange(SECTORS)
    sizes = jnp.where(index == top, M, sizes)
    sizes = jnp.where(index == bottom, M // 4, sizes)
    return sizes.astype(jnp.int32)


def draw_couplings(key, part):
    base = jax.random.fold_in(key, 23)
    first, second, third, fourth = jax.random.split(base, 4)
    counts = jax.random.randint(first, (SECTORS,), 1, KMAX + 1)
    full_row = jax.random.randint(second, (), 0, SECTORS)
    offset = jax.random.randint(third, (), 1, SECTORS)
    single_row = (full_row + offset) % SECTORS
    index = jnp.arange(SECTORS)
    counts = jnp.where(index == full_row, KMAX, counts)
    counts = jnp.where(index == single_row, 1, counts)
    row_keys = jax.random.split(fourth, SECTORS)
    orders = jax.vmap(lambda k: jax.random.permutation(k, SECTORS))(row_keys)[:, :KMAX]
    slots = jnp.arange(KMAX)[None, :]
    table = jnp.where(slots < counts[:, None], orders, -1)
    return table.astype(jnp.int32)


def level_of(key, shape, cuts, smallest, largest):
    factor_of = 1.0
    for dim, parts in cuts:
        draws = jax.random.uniform(jax.random.fold_in(jax.random.fold_in(key, 6), dim), (parts,), jnp.float32, smallest / len(cuts), largest / len(cuts))
        factor_of = factor_of * jnp.repeat(jnp.exp(draws), shape[dim] // parts).reshape((-1,) + (1,) * (len(shape) - 1 - dim))
    return factor_of


def normal_values(stream_key, dims, width, reach, cuts=(), kind=jnp.bfloat16):
    entries = width * jax.random.normal(stream_key, dims, jnp.float32)
    if cuts:
        entries = entries * level_of(stream_key, dims, cuts, -0.22, 0.18)
    return jnp.clip(entries, -reach, reach).astype(kind)


def setup_inputs(seed: int = 0) -> dict:
    streams_of = jax.random.split(jax.random.key(seed), 9)
    left_ops = normal_values(streams_of[0], (SECTORS, P_SIZE, B0, B0), 1.0, 6.0, ((0, 4), (1, 8)))
    rotation = normal_values(streams_of[1], (SECTORS, B0, M), B0 ** -0.5, 0.375, ((0, 4),))
    integrals = normal_values(streams_of[2], (P_SIZE, P_SIZE), P_SIZE ** -0.5, 0.25)
    right_ops = normal_values(streams_of[3], (SECTORS, P_SIZE, MR, MR), (M * MR * P_SIZE) ** -0.5, 0.001953125, ((0, 4), (1, 8)))
    states = normal_values(streams_of[4], (SECTORS, ROOTS, M, MR), 1.0, 6.0, ((0, 4), (2, 8)))
    sector_sizes = draw_sector_sizes(jax.random.fold_in(streams_of[8], 71), 0)
    couplings = draw_couplings(jax.random.fold_in(streams_of[8], 71), 0)
    pair_order = jax.random.permutation(streams_of[7], P_SIZE).astype(jnp.int32)
    return dict(left_ops=left_ops, rotation=rotation, integrals=integrals, right_ops=right_ops, states=states, sector_sizes=sector_sizes, couplings=couplings, pair_order=pair_order)


def reference(left_ops, rotation, integrals, right_ops, states, sector_sizes, couplings, pair_order):
    ordered = jnp.take(integrals, pair_order.astype(jnp.int32), axis=1).astype(jnp.float32)
    sector_ids = jnp.arange(SECTORS, dtype=jnp.int32)
    weights = jnp.sum((couplings[:, :, None] == sector_ids[None, None, :]).astype(jnp.float32), axis=1)
    mixed_all = jnp.einsum('st,trab->srab', weights, states.astype(jnp.float32)).astype(jnp.bfloat16)
    block = 48 if P_SIZE % 48 == 0 else P_SIZE
    count = P_SIZE // block

    def one_sector(items):
        ops, rot, size, rops, mixed = items
        live = jnp.arange(M, dtype=jnp.int32) < size
        kept = jnp.where(live[None, :], rot, jnp.zeros_like(rot))
        keptf = kept.astype(jnp.float32)
        half = jnp.einsum('pij,jk->pik', ops.astype(jnp.float32), keptf).astype(jnp.bfloat16)
        rotated = jnp.einsum('jm,pjk->pmk', keptf, half.astype(jnp.float32)).astype(jnp.bfloat16)
        complementary = jnp.einsum('qi,iab->qab', ordered, rotated.astype(jnp.float32)).astype(jnp.bfloat16)
        qblocks = complementary.reshape(count, block, M, M)
        rblocks = rops.reshape(count, block, MR, MR)
        mixedf = mixed.astype(jnp.float32)

        def accumulate(total, pieces):
            qpiece, rpiece = pieces
            image = jnp.einsum('rbd,qcd->qrbc', mixedf, rpiece.astype(jnp.float32)).astype(jnp.bfloat16)
            total = total + jnp.einsum('qab,qrbc->rac', qpiece.astype(jnp.float32), image.astype(jnp.float32))
            return total, None

        start = jnp.zeros((ROOTS, M, MR), jnp.float32)
        total, _ = lax.scan(accumulate, start, (qblocks, rblocks))
        return total

    return lax.map(one_sector, (left_ops, rotation, sector_sizes, right_ops, mixed_all))
```

```python
import functools

import jax
import jax.numpy as jnp
from jax import lax
from jax.experimental import pallas as pl
from jax.experimental.pallas import tpu as pltpu
from jax.sharding import PartitionSpec as P

MESH = pl.DeviceIdType.MESH
F32 = jnp.float32
BF16 = jnp.bfloat16


def divisor(total, most):
    return max(d for d in range(1, most + 1) if total % d == 0)


def far_first(count):
    return sorted(range(1, count), key=lambda o: -min(o, count - o))


def kernel(
    dims,
    left, rotation, integrals, right, states, sizes, couplings, order,
    out,
    lbuf, kept, kept_t, send1, recv1, rbuf, ibuf, ordered, elems, mixed_elems, send2, recv2,
    sgath, xgath, states_x, img, lhs, total, rs_send, rs_recv,
    lsem, rsem, isem, ssem_s, ssem_r, xsem_s, xsem_r, a_s, a_r, b_s, b_r, c_s, c_r,
):
    n, sectors, pairs, all_pairs, rows, width, roots, right_width, block, group, tile, kmax = dims
    me = lax.axis_index("pair")
    sec = lax.axis_index("sec")
    blocks = pairs // block
    offsets = far_first(n)

    def fetch(j):
        return pltpu.make_async_copy(
            left.at[pl.ds(j * block, block)], lbuf.at[j % 2], lsem.at[j % 2]
        )

    fetch(0).start()
    right_copy = pltpu.make_async_copy(right, rbuf, rsem)
    right_copy.start()
    integrals_copy = pltpu.make_async_copy(integrals, ibuf, isem)
    integrals_copy.start()

    barrier = pltpu.get_barrier_semaphore()
    for o in range(1, n):
        pl.semaphore_signal(barrier, inc=1, device_id={"pair": (me + o) % n}, device_id_type=MESH)
    for o in range(1, sectors):
        pl.semaphore_signal(
            barrier, inc=1, device_id={"sec": (sec + o) % sectors}, device_id_type=MESH
        )

    lane = lax.broadcasted_iota(jnp.int32, rotation.shape, 1)
    keep = jnp.where(lane < sizes[0], rotation[...].astype(F32), 0.0)
    kept[...] = keep.astype(BF16)
    kept_t[...] = keep.T.astype(BF16)

    pl.semaphore_wait(barrier, n - 1 + sectors - 1)

    def state_copy(o):
        return pltpu.make_async_remote_copy(
            src_ref=states, dst_ref=sgath.at[sec], send_sem=ssem_s.at[o], recv_sem=ssem_r.at[o],
            device_id={"sec": (sec + o) % sectors}, device_id_type=MESH,
        )

    for o in range(1, sectors):
        state_copy(o).start()

    def elem_copy(j, o):
        dst = (me + o) % n
        return pltpu.make_async_remote_copy(
            src_ref=send1.at[dst, pl.ds(j * block, block)],
            dst_ref=recv1.at[pl.ds(me * pairs + j * block, block)],
            send_sem=a_s.at[j, o], recv_sem=a_r.at[j, o],
            device_id={"pair": dst}, device_id_type=MESH,
        )

    def left_block(j):
        @pl.when(j + 1 < blocks)
        def _():
            fetch(j + 1).start()

        fetch(j).wait()
        for i in range(block):
            half = jnp.dot(lbuf[j % 2, i], kept[...], preferred_element_type=F32).astype(BF16)
            turned = jnp.dot(kept_t[...], half, preferred_element_type=F32)
            send1[:, j * block + i] = turned.reshape(n, rows, width).astype(BF16)
        recv1[pl.ds(me * pairs + j * block, block)] = send1[me, pl.ds(j * block, block)]
        for o in offsets:
            elem_copy(j, o).start()

    def mixed_copy(o):
        return pltpu.make_async_remote_copy(
            src_ref=xgath.at[me], dst_ref=xgath.at[me], send_sem=xsem_s.at[o],
            recv_sem=xsem_r.at[o], device_id={"pair": (me + o) % n}, device_id_type=MESH,
        )

    left_block(0)
    sgath[sec] = states[...]
    for o in range(1, sectors):
        state_copy(o).wait()
    acc = jnp.zeros(states.shape, F32)
    for t in range(sectors):
        weight = jnp.int32(0)
        for k in range(kmax):
            weight = weight + jnp.where(couplings[0, k] == t, 1, 0)
        acc = acc + weight.astype(F32) * sgath[t].astype(F32)
    xgath[me] = acc.astype(BF16)
    for o in offsets:
        mixed_copy(o).start()

    @pl.loop(1, blocks)
    def _(j):
        left_block(j)

    integrals_copy.wait()
    rows_of = lax.broadcasted_iota(jnp.int32, (all_pairs, all_pairs), 0)
    pick = (rows_of == order[...]).astype(F32).astype(BF16)
    ordered[...] = jnp.dot(ibuf[...], pick, preferred_element_type=F32).astype(BF16)

    for o in offsets:
        mixed_copy(o).wait()

    @pl.loop(0, roots)
    def _(r):
        states_x[r] = xgath[:, r].reshape(n * rows, right_width)

    right_copy.wait()

    @pl.loop(0, pairs // group)
    def _(g):
        rhs = rbuf[pl.ds(g * group, group)].reshape(group * right_width, right_width)
        for r in range(roots):
            image = lax.dot_general(
                states_x[r], rhs, (((1,), (1,)), ((), ())), preferred_element_type=F32
            ).astype(BF16)
            for k in range(group):
                img[g * group + k, :, r * right_width:(r + 1) * right_width] = image[
                    :, k * right_width:(k + 1) * right_width
                ]

    size = tile * rows
    at = lax.broadcasted_iota(jnp.int32, (size, size), 0)
    to = lax.broadcasted_iota(jnp.int32, (size, size), 1)
    forth = (to == (at % tile) * rows + at // tile).astype(F32).astype(BF16)
    back = (to == (at % rows) * tile + at // rows).astype(F32).astype(BF16)

    @pl.loop(0, blocks)
    def _(j):
        for o in offsets:
            elem_copy(j, o).wait()

    @pl.loop(0, all_pairs // tile)
    def _(b):
        piece = recv1[pl.ds(b * tile, tile)].reshape(size, width)
        piece = jnp.dot(forth, piece, preferred_element_type=F32).astype(BF16)
        at_b = pl.multiple_of(b * tile, tile)
        for m in range(rows):
            elems[pl.ds(at_b, tile), m * width:(m + 1) * width] = piece[m * tile:(m + 1) * tile]

    span = 2 * width

    @pl.loop(0, rows * width // span)
    def _(c):
        cols = pl.ds(pl.multiple_of(c * span, span), span)
        mixed_elems[:, cols] = jnp.dot(
            ordered[...], elems[:, cols], preferred_element_type=F32
        ).astype(BF16)

    @pl.loop(0, all_pairs // tile)
    def _(b):
        at_b = pl.multiple_of(b * tile, tile)
        piece = jnp.concatenate(
            [mixed_elems[pl.ds(at_b, tile), m * width:(m + 1) * width] for m in range(rows)], axis=0
        )
        piece = jnp.dot(back, piece, preferred_element_type=F32)
        send2[pl.ds(b * tile, tile)] = piece.reshape(tile, rows, width).astype(BF16)

    def back_copy(j, o):
        dst = (me + o) % n
        return pltpu.make_async_remote_copy(
            src_ref=send2.at[pl.ds(dst * pairs + j * block, block)],
            dst_ref=recv2.at[me, pl.ds(j * block, block)],
            send_sem=b_s.at[j, o], recv_sem=b_r.at[j, o],
            device_id={"pair": dst}, device_id_type=MESH,
        )

    @pl.loop(0, blocks)
    def _(j):
        for o in offsets:
            back_copy(j, o).start()

    recv2[me] = send2[pl.ds(me * pairs, pairs)]
    total[...] = jnp.zeros_like(total)

    @pl.loop(0, blocks)
    def _(j):
        for o in offsets:
            back_copy(j, o).wait()
        for i in range(block):
            lhs[:, i * width:(i + 1) * width] = recv2[:, j * block + i].reshape(n * rows, width)

        @pl.loop(0, roots * right_width // span)
        def _(c):
            cols = pl.ds(pl.multiple_of(c * span, span), span)
            total[:, cols] += jnp.dot(
                lhs[...],
                img[pl.ds(j * block, block), :, cols].reshape(block * width, span),
                preferred_element_type=F32,
            )

    rs_send[...] = total[...].reshape(n, rows, roots * right_width).astype(BF16)

    def sum_copy(o):
        dst = (me + o) % n
        return pltpu.make_async_remote_copy(
            src_ref=rs_send.at[dst], dst_ref=rs_recv.at[o], send_sem=c_s.at[o],
            recv_sem=c_r.at[o], device_id={"pair": dst}, device_id_type=MESH,
        )

    for o in offsets:
        sum_copy(o).start()
    mine = total[pl.ds(pl.multiple_of(me * rows, rows), rows), :]
    for o in reversed(offsets):
        sum_copy(o).wait()
        mine = mine + rs_recv[o].astype(F32)
    for r in range(roots):
        out[r] = mine[:, r * right_width:(r + 1) * right_width]


def local(n, sectors, left_ops, rotation, integrals, right_ops, states, sector_sizes, couplings,
          pair_order):
    left_ops, rotation, right_ops, states = left_ops[0], rotation[0], right_ops[0], states[0]
    pairs, basis, _ = left_ops.shape
    width = rotation.shape[1]
    all_pairs = integrals.shape[0]
    roots, rows, right_width = states.shape
    block = divisor(pairs, 11)
    group = 2 if pairs % 2 == 0 else divisor(pairs, 3)
    tile = divisor(all_pairs, 16)
    blocks = pairs // block
    dims = (n, sectors, pairs, all_pairs, rows, width, roots, right_width, block, group, tile,
            couplings.shape[1])
    vmem = pl.BlockSpec(memory_space=pltpu.VMEM)
    smem = pl.BlockSpec(memory_space=pltpu.SMEM)
    anywhere = pl.BlockSpec(memory_space=pl.ANY)
    dma = pltpu.SemaphoreType.DMA
    sigma = pl.pallas_call(
        functools.partial(kernel, dims),
        out_shape=jax.ShapeDtypeStruct((roots, rows, right_width), F32),
        in_specs=[anywhere, vmem, anywhere, anywhere, vmem, smem, smem, vmem],
        out_specs=vmem,
        scratch_shapes=[
            pltpu.VMEM((2, block, basis, basis), BF16),
            pltpu.VMEM((basis, width), BF16),
            pltpu.VMEM((width, basis), BF16),
            pltpu.VMEM((n, pairs, rows, width), BF16),
            pltpu.VMEM((all_pairs, rows, width), BF16),
            pltpu.VMEM((pairs, right_width, right_width), BF16),
            pltpu.VMEM((all_pairs, all_pairs), BF16),
            pltpu.VMEM((all_pairs, all_pairs), BF16),
            pltpu.VMEM((all_pairs, rows * width), BF16),
            pltpu.VMEM((all_pairs, rows * width), BF16),
            pltpu.VMEM((all_pairs, rows, width), BF16),
            pltpu.VMEM((n, pairs, rows, width), BF16),
            pltpu.VMEM((sectors, roots, rows, right_width), BF16),
            pltpu.VMEM((n, roots, rows, right_width), BF16),
            pltpu.VMEM((roots, n * rows, right_width), BF16),
            pltpu.VMEM((pairs, width, roots * right_width), BF16),
            pltpu.VMEM((n * rows, block * width), BF16),
            pltpu.VMEM((n * rows, roots * right_width), F32),
            pltpu.VMEM((n, rows, roots * right_width), BF16),
            pltpu.VMEM((n, rows, roots * right_width), BF16),
            dma((2,)), dma, dma,
            dma((sectors,)), dma((sectors,)),
            dma((n,)), dma((n,)),
            dma((blocks, n)), dma((blocks, n)),
            dma((blocks, n)), dma((blocks, n)),
            dma((n,)), dma((n,)),
        ],
        compiler_params=pltpu.CompilerParams(
            collective_id=0, has_side_effects=True, vmem_limit_bytes=67043328
        ),
    )(left_ops, rotation, integrals, right_ops, states, sector_sizes, couplings,
      pair_order[None, :])
    return sigma[None]


def solution(mesh):
    placed = (
        P("sec", "pair", None, None),
        P("sec", None, None),
        P(),
        P("sec", "pair", None, None),
        P("sec", None, "pair", None),
        P("sec"),
        P("sec", None),
        P(),
    )
    return jax.shard_map(
        functools.partial(local, mesh.shape["pair"], mesh.shape["sec"]),
        mesh=mesh, in_specs=placed, out_specs=P("sec", None, "pair", None), check_vma=False,
    )
```

```python
import functools

import jax
import jax.numpy as jnp
from jax import lax
from jax.experimental import pallas as pl
from jax.experimental.pallas import tpu as pltpu
from jax.sharding import PartitionSpec as P

MESH = pl.DeviceIdType.MESH
F32 = jnp.float32
BF16 = jnp.bfloat16


def divisor(total, most):
    return max(d for d in range(1, most + 1) if total % d == 0)


def far_first(count):
    return sorted(range(1, count), key=lambda o: -min(o, count - o))


def kernel(
    dims,
    left, rotation, integrals, right, states, sizes, couplings, order,
    out,
    lbuf, kept, kept_t, send1, recv1, rbuf, ibuf, ordered, elems, mixed_elems, send2, recv2,
    sgath, xgath, states_x, img, lhs, total, rs_send, rs_pre, rs_part, rs_recv,
    lsem, rsem, isem, ssem_s, ssem_r, xsem_s, xsem_r, a_s, a_r, b_s, b_r, p_s, p_r, c_s, c_r,
):
    n, sectors, pairs, all_pairs, rows, width, roots, right_width, block, group, tile, kmax, chunk = dims
    chunks = rows // chunk
    me = lax.axis_index("pair")
    sec = lax.axis_index("sec")
    blocks = pairs // block
    offsets = far_first(n)

    def fetch(j):
        return pltpu.make_async_copy(
            left.at[pl.ds(j * block, block)], lbuf.at[j % 2], lsem.at[j % 2]
        )

    fetch(0).start()
    right_copy = pltpu.make_async_copy(right, rbuf, rsem)
    right_copy.start()
    integrals_copy = pltpu.make_async_copy(integrals, ibuf, isem)
    integrals_copy.start()

    barrier = pltpu.get_barrier_semaphore()
    for o in range(1, n):
        pl.semaphore_signal(barrier, inc=1, device_id={"pair": (me + o) % n}, device_id_type=MESH)
    for o in range(1, sectors):
        pl.semaphore_signal(
            barrier, inc=1, device_id={"sec": (sec + o) % sectors}, device_id_type=MESH
        )

    lane = lax.broadcasted_iota(jnp.int32, rotation.shape, 1)
    keep = jnp.where(lane < sizes[0], rotation[...].astype(F32), 0.0)
    kept[...] = keep.astype(BF16)
    kept_t[...] = keep.T.astype(BF16)

    pl.semaphore_wait(barrier, n - 1 + sectors - 1)

    def state_copy(o):
        return pltpu.make_async_remote_copy(
            src_ref=states, dst_ref=sgath.at[sec], send_sem=ssem_s.at[o], recv_sem=ssem_r.at[o],
            device_id={"sec": (sec + o) % sectors}, device_id_type=MESH,
        )

    for o in range(1, sectors):
        state_copy(o).start()

    def elem_copy(c, j, o, length):
        dst = (me + o) % n
        return pltpu.make_async_remote_copy(
            src_ref=send1.at[c, dst, pl.ds(j * block, length)],
            dst_ref=recv1.at[c, pl.ds(me * pairs + j * block, length)],
            send_sem=a_s.at[c, j, o], recv_sem=a_r.at[c, j, o],
            device_id={"pair": dst}, device_id_type=MESH,
        )

    def left_block(j):
        @pl.when(j + 1 < blocks)
        def _():
            fetch(j + 1).start()

        fetch(j).wait()
        for i in range(block):
            half = jnp.dot(lbuf[j % 2, i], kept[...], preferred_element_type=F32).astype(BF16)
            turned = jnp.dot(kept_t[...], half, preferred_element_type=F32)
            turned = turned.reshape(n, chunks, chunk, width)
            for c in range(chunks):
                send1[c, :, j * block + i] = turned[:, c].astype(BF16)
        for c in range(chunks):
            recv1[c, pl.ds(me * pairs + j * block, block)] = send1[c, me, pl.ds(j * block, block)]
        for o in offsets:
            elem_copy(0, j, o, block).start()

    def mixed_copy(o):
        return pltpu.make_async_remote_copy(
            src_ref=xgath.at[me], dst_ref=xgath.at[me], send_sem=xsem_s.at[o],
            recv_sem=xsem_r.at[o], device_id={"pair": (me + o) % n}, device_id_type=MESH,
        )

    left_block(0)
    sgath[sec] = states[...]
    for o in range(1, sectors):
        state_copy(o).wait()
    acc = jnp.zeros(states.shape, F32)
    for t in range(sectors):
        weight = jnp.int32(0)
        for k in range(kmax):
            weight = weight + jnp.where(couplings[0, k] == t, 1, 0)
        acc = acc + weight.astype(F32) * sgath[t].astype(F32)
    xgath[me] = acc.astype(BF16)
    for o in offsets:
        mixed_copy(o).start()

    @pl.loop(1, blocks)
    def _(j):
        left_block(j)

    for c in range(1, chunks):
        for o in offsets:
            elem_copy(c, 0, o, pairs).start()

    integrals_copy.wait()
    rows_of = lax.broadcasted_iota(jnp.int32, (all_pairs, all_pairs), 0)
    pick = (rows_of == order[...]).astype(F32).astype(BF16)
    ordered[...] = jnp.dot(ibuf[...], pick, preferred_element_type=F32).astype(BF16)

    for o in offsets:
        mixed_copy(o).wait()

    @pl.loop(0, roots)
    def _(r):
        states_x[r] = xgath[:, r].reshape(n * rows, right_width)

    right_copy.wait()

    @pl.loop(0, pairs // group)
    def _(g):
        rhs = rbuf[pl.ds(g * group, group)].reshape(group * right_width, right_width)
        for r in range(roots):
            image = lax.dot_general(
                states_x[r], rhs, (((1,), (1,)), ((), ())), preferred_element_type=F32
            ).astype(BF16)
            for k in range(group):
                img[g * group + k, :, r * right_width:(r + 1) * right_width] = image[
                    :, k * right_width:(k + 1) * right_width
                ]

    size = tile * chunk
    at = lax.broadcasted_iota(jnp.int32, (size, size), 0)
    to = lax.broadcasted_iota(jnp.int32, (size, size), 1)
    forth = (to == (at % tile) * chunk + at // tile).astype(F32).astype(BF16)
    back = (to == (at % chunk) * tile + at // chunk).astype(F32).astype(BF16)
    tiles = all_pairs // tile
    batch = divisor(tiles, 11)
    span = 2 * width

    def back_copy(c, j, o, length):
        dst = (me + o) % n
        return pltpu.make_async_remote_copy(
            src_ref=send2.at[c, pl.ds(dst * pairs + j * block, length)],
            dst_ref=recv2.at[c, me, pl.ds(j * block, length)],
            send_sem=b_s.at[c, j, o], recv_sem=b_r.at[c, j, o],
            device_id={"pair": dst}, device_id_type=MESH,
        )

    for c in range(chunks):
        if c == 0:
            @pl.loop(0, blocks)
            def _(j):
                for o in offsets:
                    elem_copy(0, j, o, block).wait()
        else:
            for o in offsets:
                elem_copy(c, 0, o, pairs).wait()

        @pl.loop(0, tiles // batch)
        def _(b):
            piece = jnp.concatenate(
                [recv1[c, pl.ds((b * batch + k) * tile, tile)].reshape(size, width)
                 for k in range(batch)], axis=1
            )
            piece = jnp.dot(forth, piece, preferred_element_type=F32).astype(BF16)
            for k in range(batch):
                at_b = pl.multiple_of((b * batch + k) * tile, tile)
                for m in range(chunk):
                    elems[pl.ds(at_b, tile), m * width:(m + 1) * width] = piece[
                        m * tile:(m + 1) * tile, k * width:(k + 1) * width
                    ]

        @pl.loop(0, chunk * width // span)
        def _(g):
            cols = pl.ds(pl.multiple_of(g * span, span), span)
            mixed_elems[:, cols] = jnp.dot(
                ordered[...], elems[:, cols], preferred_element_type=F32
            ).astype(BF16)

        @pl.loop(0, tiles // batch)
        def _(b):
            pieces = []
            for k in range(batch):
                at_b = pl.multiple_of((b * batch + k) * tile, tile)
                pieces.append(jnp.concatenate(
                    [mixed_elems[pl.ds(at_b, tile), m * width:(m + 1) * width]
                     for m in range(chunk)], axis=0
                ))
            piece = jnp.dot(back, jnp.concatenate(pieces, axis=1), preferred_element_type=F32)
            for k in range(batch):
                send2[c, pl.ds((b * batch + k) * tile, tile)] = piece[
                    :, k * width:(k + 1) * width
                ].reshape(tile, chunk, width).astype(BF16)

        if c < chunks - 1:
            for o in offsets:
                back_copy(c, 0, o, pairs).start()
        else:
            @pl.loop(0, blocks)
            def _(j):
                for o in offsets:
                    back_copy(c, j, o, block).start()

        recv2[c, me] = send2[c, pl.ds(me * pairs, pairs)]

    total[...] = jnp.zeros_like(total)

    for c in range(chunks - 1):
        for o in offsets:
            back_copy(c, 0, o, pairs).wait()

    @pl.loop(0, blocks)
    def _(j):
        for o in offsets:
            back_copy(chunks - 1, j, o, block).wait()
        for i in range(block):
            for c in range(chunks):
                lhs[c * n * chunk:(c + 1) * n * chunk, i * width:(i + 1) * width] = recv2[
                    c, :, j * block + i
                ].reshape(n * chunk, width)

        @pl.loop(0, roots * right_width // span)
        def _(c):
            cols = pl.ds(pl.multiple_of(c * span, span), span)
            total[:, cols] += jnp.dot(
                lhs[...],
                img[pl.ds(j * block, block), :, cols].reshape(block * width, span),
                preferred_element_type=F32,
            )

    core = me % 2
    chip = me // 2
    chips = n // 2
    for d in range(n):
        for c in range(chunks):
            first = (c * n + d) * chunk
            rs_send[d % 2, d // 2, c] = total[first:first + chunk, :].astype(BF16)
    near = pltpu.make_async_remote_copy(
        src_ref=rs_send.at[1 - core], dst_ref=rs_pre, send_sem=p_s, recv_sem=p_r,
        device_id={"pair": chip * 2 + 1 - core}, device_id_type=MESH,
    )
    near.start()
    near.wait()

    def part(z, c):
        first = pl.multiple_of((c * n + 2 * z + core) * chunk, chunk)
        return total[pl.ds(first, chunk), :] + rs_pre[z, c].astype(F32)

    def sum_copy(o):
        dst = (chip + o) % chips
        return pltpu.make_async_remote_copy(
            src_ref=rs_part.at[o], dst_ref=rs_recv.at[o], send_sem=c_s.at[o],
            recv_sem=c_r.at[o], device_id={"pair": dst * 2 + core}, device_id_type=MESH,
        )

    far = far_first(chips)
    for o in far:
        for c in range(chunks):
            rs_part[o, c] = part((chip + o) % chips, c).astype(BF16)
        sum_copy(o).start()
    for c in range(chunks):
        total[c * chunk:(c + 1) * chunk, :] = part(chip, c)
    for o in far:
        sum_copy(o).wait()
    for c in range(chunks):
        mine = total[c * chunk:(c + 1) * chunk, :]
        for o in far:
            mine = mine + rs_recv[o, c].astype(F32)
        for r in range(roots):
            out[r, c * chunk:(c + 1) * chunk] = mine[:, r * right_width:(r + 1) * right_width]


def local(n, sectors, left_ops, rotation, integrals, right_ops, states, sector_sizes, couplings,
          pair_order):
    left_ops, rotation, right_ops, states = left_ops[0], rotation[0], right_ops[0], states[0]
    pairs, basis, _ = left_ops.shape
    width = rotation.shape[1]
    all_pairs = integrals.shape[0]
    roots, rows, right_width = states.shape
    block = divisor(pairs, 11)
    group = 2 if pairs % 2 == 0 else divisor(pairs, 3)
    tile = divisor(all_pairs, 16)
    blocks = pairs // block
    chunk = 8 if rows % 8 == 0 else rows
    chunks = rows // chunk
    dims = (n, sectors, pairs, all_pairs, rows, width, roots, right_width, block, group, tile,
            couplings.shape[1], chunk)
    vmem = pl.BlockSpec(memory_space=pltpu.VMEM)
    smem = pl.BlockSpec(memory_space=pltpu.SMEM)
    anywhere = pl.BlockSpec(memory_space=pl.ANY)
    dma = pltpu.SemaphoreType.DMA
    sigma = pl.pallas_call(
        functools.partial(kernel, dims),
        out_shape=jax.ShapeDtypeStruct((roots, rows, right_width), F32),
        in_specs=[anywhere, vmem, anywhere, anywhere, vmem, smem, smem, vmem],
        out_specs=vmem,
        scratch_shapes=[
            pltpu.VMEM((2, block, basis, basis), BF16),
            pltpu.VMEM((basis, width), BF16),
            pltpu.VMEM((width, basis), BF16),
            pltpu.VMEM((chunks, n, pairs, chunk, width), BF16),
            pltpu.VMEM((chunks, all_pairs, chunk, width), BF16),
            pltpu.VMEM((pairs, right_width, right_width), BF16),
            pltpu.VMEM((all_pairs, all_pairs), BF16),
            pltpu.VMEM((all_pairs, all_pairs), BF16),
            pltpu.VMEM((all_pairs, chunk * width), BF16),
            pltpu.VMEM((all_pairs, chunk * width), BF16),
            pltpu.VMEM((chunks, all_pairs, chunk, width), BF16),
            pltpu.VMEM((chunks, n, pairs, chunk, width), BF16),
            pltpu.VMEM((sectors, roots, rows, right_width), BF16),
            pltpu.VMEM((n, roots, rows, right_width), BF16),
            pltpu.VMEM((roots, n * rows, right_width), BF16),
            pltpu.VMEM((pairs, width, roots * right_width), BF16),
            pltpu.VMEM((n * rows, block * width), BF16),
            pltpu.VMEM((n * rows, roots * right_width), F32),
            pltpu.VMEM((2, n // 2, chunks, chunk, roots * right_width), BF16),
            pltpu.VMEM((n // 2, chunks, chunk, roots * right_width), BF16),
            pltpu.VMEM((n // 2, chunks, chunk, roots * right_width), BF16),
            pltpu.VMEM((n // 2, chunks, chunk, roots * right_width), BF16),
            dma((2,)), dma, dma,
            dma((sectors,)), dma((sectors,)),
            dma((n,)), dma((n,)),
            dma((chunks, blocks, n)), dma((chunks, blocks, n)),
            dma((chunks, blocks, n)), dma((chunks, blocks, n)),
            dma, dma,
            dma((n // 2,)), dma((n // 2,)),
        ],
        compiler_params=pltpu.CompilerParams(
            collective_id=0, has_side_effects=True, vmem_limit_bytes=67043328
        ),
    )(left_ops, rotation, integrals, right_ops, states, sector_sizes, couplings,
      pair_order[None, :])
    return sigma[None]


def solution(mesh):
    placed = (
        P("sec", "pair", None, None),
        P("sec", None, None),
        P(),
        P("sec", "pair", None, None),
        P("sec", None, "pair", None),
        P("sec"),
        P("sec", None),
        P(),
    )
    return jax.shard_map(
        functools.partial(local, mesh.shape["pair"], mesh.shape["sec"]),
        mesh=mesh, in_specs=placed, out_specs=P("sec", None, "pair", None), check_vma=False,
    )
```

```python
import functools

import jax
import jax.numpy as jnp
from jax import lax
from jax.experimental import pallas as pl
from jax.experimental.pallas import tpu as pltpu
from jax.sharding import PartitionSpec as P

MESH = pl.DeviceIdType.MESH
F32 = jnp.float32
BF16 = jnp.bfloat16


def divisor(total, most):
    return max(d for d in range(1, most + 1) if total % d == 0)


def partners(count):
    return list(range(1, count))


def kernel(
    dims,
    left, rotation, integrals, right, states, sizes, couplings, order,
    out,
    lbuf, kept, kept_t, send1, recv1, rbuf, ibuf, ordered, elems, mixed_elems, send2, recv2,
    sgath, xgath, states_x, img, lhs, total, rs_send, rs_pre, rs_part, rs_recv,
    lsem, rsem, isem, ssem_s, ssem_r, xsem_s, xsem_r, a_s, a_r, b_s, b_r, p_s, p_r, c_s, c_r,
):
    n, sectors, pairs, all_pairs, rows, width, roots, right_width, block, group, tile, kmax, chunk = dims
    chunks = rows // chunk
    me = lax.axis_index("pair")
    sec = lax.axis_index("sec")
    blocks = pairs // block
    offsets = partners(n)

    def fetch(j):
        return pltpu.make_async_copy(
            left.at[pl.ds(j * block, block)], lbuf.at[j % 2], lsem.at[j % 2]
        )

    fetch(0).start()
    right_copy = pltpu.make_async_copy(right, rbuf, rsem)
    right_copy.start()
    integrals_copy = pltpu.make_async_copy(integrals, ibuf, isem)
    integrals_copy.start()

    barrier = pltpu.get_barrier_semaphore()
    for o in range(1, n):
        pl.semaphore_signal(barrier, inc=1, device_id={"pair": (me + o) % n}, device_id_type=MESH)
    for o in range(1, sectors):
        pl.semaphore_signal(
            barrier, inc=1, device_id={"sec": (sec + o) % sectors}, device_id_type=MESH
        )

    lane = lax.broadcasted_iota(jnp.int32, rotation.shape, 1)
    keep = jnp.where(lane < sizes[0], rotation[...].astype(F32), 0.0)
    kept[...] = keep.astype(BF16)
    kept_t[...] = keep.T.astype(BF16)

    pl.semaphore_wait(barrier, n - 1 + sectors - 1)

    def state_copy(o):
        return pltpu.make_async_remote_copy(
            src_ref=states, dst_ref=sgath.at[sec], send_sem=ssem_s.at[o], recv_sem=ssem_r.at[o],
            device_id={"sec": (sec + o) % sectors}, device_id_type=MESH,
        )

    for o in range(1, sectors):
        state_copy(o).start()

    def elem_copy(c, j, o, length):
        dst = (me + o) % n
        return pltpu.make_async_remote_copy(
            src_ref=send1.at[c, dst, pl.ds(j * block, length)],
            dst_ref=recv1.at[c, pl.ds(me * pairs + j * block, length)],
            send_sem=a_s.at[c, j, o], recv_sem=a_r.at[c, j, o],
            device_id={"pair": dst}, device_id_type=MESH,
        )

    def left_block(j):
        if isinstance(j, int):
            if j + 1 < blocks:
                fetch(j + 1).start()
        else:
            @pl.when(j + 1 < blocks)
            def _():
                fetch(j + 1).start()

        fetch(j).wait()
        for i in range(block):
            half = jnp.dot(lbuf[j % 2, i], kept[...], preferred_element_type=F32).astype(BF16)
            turned = jnp.dot(kept_t[...], half, preferred_element_type=F32)
            turned = turned.reshape(n, chunks, chunk, width)
            for c in range(chunks):
                send1[c, :, j * block + i] = turned[:, c].astype(BF16)
        for c in range(chunks):
            recv1[c, pl.ds(me * pairs + j * block, block)] = send1[c, me, pl.ds(j * block, block)]
        for o in offsets:
            elem_copy(0, j, o, block).start()

    def mixed_copy(o):
        return pltpu.make_async_remote_copy(
            src_ref=xgath.at[me], dst_ref=xgath.at[me], send_sem=xsem_s.at[o],
            recv_sem=xsem_r.at[o], device_id={"pair": (me + o) % n}, device_id_type=MESH,
        )

    lead = min(3, blocks)
    for j in range(lead):
        left_block(j)
    sgath[sec] = states[...]
    for o in range(1, sectors):
        state_copy(o).wait()
    acc = jnp.zeros(states.shape, F32)
    for t in range(sectors):
        weight = jnp.int32(0)
        for k in range(kmax):
            weight = weight + jnp.where(couplings[0, k] == t, 1, 0)
        acc = acc + weight.astype(F32) * sgath[t].astype(F32)
    xgath[me] = acc.astype(BF16)
    for o in offsets:
        mixed_copy(o).start()

    @pl.loop(lead, blocks)
    def _(j):
        left_block(j)

    for c in range(1, chunks):
        for o in offsets:
            elem_copy(c, 0, o, pairs).start()

    integrals_copy.wait()
    rows_of = lax.broadcasted_iota(jnp.int32, (all_pairs, all_pairs), 0)
    pick = (rows_of == order[...][None, :]).astype(F32).astype(BF16)
    ordered[...] = jnp.dot(ibuf[...], pick, preferred_element_type=F32).astype(BF16)

    def images():
        for o in offsets:
            mixed_copy(o).wait()

        @pl.loop(0, roots)
        def _(r):
            states_x[r] = xgath[:, r].reshape(n * rows, right_width)

        right_copy.wait()

        @pl.loop(0, pairs // group)
        def _(g):
            rhs = rbuf[pl.ds(g * group, group)].reshape(group * right_width, right_width)
            for r in range(roots):
                image = lax.dot_general(
                    states_x[r], rhs, (((1,), (1,)), ((), ())), preferred_element_type=F32
                ).astype(BF16)
                for k in range(group):
                    img[g * group + k, :, r * right_width:(r + 1) * right_width] = image[
                        :, k * right_width:(k + 1) * right_width
                    ]

    size = tile * chunk
    at = lax.broadcasted_iota(jnp.int32, (size, size), 0)
    to = lax.broadcasted_iota(jnp.int32, (size, size), 1)
    forth = (to == (at % tile) * chunk + at // tile).astype(F32).astype(BF16)
    back = (to == (at % chunk) * tile + at // chunk).astype(F32).astype(BF16)
    tiles = all_pairs // tile
    batch = divisor(tiles, 11)
    span = 2 * width

    def back_copy(c, j, o, length):
        dst = (me + o) % n
        return pltpu.make_async_remote_copy(
            src_ref=send2.at[c, pl.ds(dst * pairs + j * block, length)],
            dst_ref=recv2.at[c, me, pl.ds(j * block, length)],
            send_sem=b_s.at[c, j, o], recv_sem=b_r.at[c, j, o],
            device_id={"pair": dst}, device_id_type=MESH,
        )

    if chunks == 1:
        images()

    for c in range(chunks):
        if c == 0:
            @pl.loop(0, blocks)
            def _(j):
                for o in offsets:
                    elem_copy(0, j, o, block).wait()
        else:
            for o in offsets:
                elem_copy(c, 0, o, pairs).wait()

        @pl.loop(0, tiles // batch)
        def _(b):
            piece = jnp.concatenate(
                [recv1[c, pl.ds((b * batch + k) * tile, tile)].reshape(size, width)
                 for k in range(batch)], axis=1
            )
            piece = jnp.dot(forth, piece, preferred_element_type=F32).astype(BF16)
            for k in range(batch):
                at_b = pl.multiple_of((b * batch + k) * tile, tile)
                for m in range(chunk):
                    elems[pl.ds(at_b, tile), m * width:(m + 1) * width] = piece[
                        m * tile:(m + 1) * tile, k * width:(k + 1) * width
                    ]

        @pl.loop(0, chunk * width // span)
        def _(g):
            cols = pl.ds(pl.multiple_of(g * span, span), span)
            mixed_elems[:, cols] = jnp.dot(
                ordered[...], elems[:, cols], preferred_element_type=F32
            ).astype(BF16)

        @pl.loop(0, tiles // batch)
        def _(b):
            pieces = []
            for k in range(batch):
                at_b = pl.multiple_of((b * batch + k) * tile, tile)
                pieces.append(jnp.concatenate(
                    [mixed_elems[pl.ds(at_b, tile), m * width:(m + 1) * width]
                     for m in range(chunk)], axis=0
                ))
            piece = jnp.dot(back, jnp.concatenate(pieces, axis=1), preferred_element_type=F32)
            for k in range(batch):
                send2[c, pl.ds((b * batch + k) * tile, tile)] = piece[
                    :, k * width:(k + 1) * width
                ].reshape(tile, chunk, width).astype(BF16)

        if c < chunks - 1:
            for o in offsets:
                back_copy(c, 0, o, pairs).start()
            if c == 0:
                images()
        else:
            @pl.loop(0, blocks)
            def _(j):
                for o in offsets:
                    back_copy(c, j, o, block).start()

        recv2[c, me] = send2[c, pl.ds(me * pairs, pairs)]

    total[...] = jnp.zeros_like(total)

    for c in range(chunks - 1):
        for o in offsets:
            back_copy(c, 0, o, pairs).wait()

    @pl.loop(0, blocks)
    def _(j):
        for o in offsets:
            back_copy(chunks - 1, j, o, block).wait()
        for i in range(block):
            for c in range(chunks):
                lhs[c * n * chunk:(c + 1) * n * chunk, i * width:(i + 1) * width] = recv2[
                    c, :, j * block + i
                ].reshape(n * chunk, width)

        @pl.loop(0, roots * right_width // span)
        def _(c):
            cols = pl.ds(pl.multiple_of(c * span, span), span)
            total[:, cols] += jnp.dot(
                lhs[...],
                img[pl.ds(j * block, block), :, cols].reshape(block * width, span),
                preferred_element_type=F32,
            )

    core = me % 2
    chip = me // 2
    chips = n // 2
    for d in range(n):
        for c in range(chunks):
            first = (c * n + d) * chunk
            rs_send[d % 2, d // 2, c] = total[first:first + chunk, :].astype(BF16)
    near = pltpu.make_async_remote_copy(
        src_ref=rs_send.at[1 - core], dst_ref=rs_pre, send_sem=p_s, recv_sem=p_r,
        device_id={"pair": chip * 2 + 1 - core}, device_id_type=MESH,
    )
    near.start()
    near.wait()

    def part(z, c):
        first = pl.multiple_of((c * n + 2 * z + core) * chunk, chunk)
        return total[pl.ds(first, chunk), :] + rs_pre[z, c].astype(F32)

    def sum_copy(o):
        dst = (chip + o) % chips
        return pltpu.make_async_remote_copy(
            src_ref=rs_part.at[o], dst_ref=rs_recv.at[o], send_sem=c_s.at[o],
            recv_sem=c_r.at[o], device_id={"pair": dst * 2 + core}, device_id_type=MESH,
        )

    far = partners(chips)
    for o in far:
        for c in range(chunks):
            rs_part[o, c] = part((chip + o) % chips, c).astype(BF16)
        sum_copy(o).start()
    for c in range(chunks):
        total[c * chunk:(c + 1) * chunk, :] = part(chip, c)
    for o in far:
        sum_copy(o).wait()
    for c in range(chunks):
        mine = total[c * chunk:(c + 1) * chunk, :]
        for o in far:
            mine = mine + rs_recv[o, c].astype(F32)
        for r in range(roots):
            out[r, c * chunk:(c + 1) * chunk] = mine[:, r * right_width:(r + 1) * right_width]


def local(n, sectors, left_ops, rotation, integrals, right_ops, states, sector_sizes, couplings,
          pair_order):
    left_ops, rotation, right_ops, states = left_ops[0], rotation[0], right_ops[0], states[0]
    pairs, basis, _ = left_ops.shape
    width = rotation.shape[1]
    all_pairs = integrals.shape[0]
    roots, rows, right_width = states.shape
    block = divisor(pairs, 11)
    group = 2 if pairs % 2 == 0 else divisor(pairs, 3)
    tile = divisor(all_pairs, 16)
    blocks = pairs // block
    chunk = 8 if rows % 8 == 0 else rows
    chunks = rows // chunk
    dims = (n, sectors, pairs, all_pairs, rows, width, roots, right_width, block, group, tile,
            couplings.shape[1], chunk)
    vmem = pl.BlockSpec(memory_space=pltpu.VMEM)
    smem = pl.BlockSpec(memory_space=pltpu.SMEM)
    anywhere = pl.BlockSpec(memory_space=pl.ANY)
    dma = pltpu.SemaphoreType.DMA
    sigma = pl.pallas_call(
        functools.partial(kernel, dims),
        out_shape=jax.ShapeDtypeStruct((roots, rows, right_width), F32),
        in_specs=[anywhere, vmem, anywhere, anywhere, vmem, smem, smem, vmem],
        out_specs=vmem,
        scratch_shapes=[
            pltpu.VMEM((2, block, basis, basis), BF16),
            pltpu.VMEM((basis, width), BF16),
            pltpu.VMEM((width, basis), BF16),
            pltpu.VMEM((chunks, n, pairs, chunk, width), BF16),
            pltpu.VMEM((chunks, all_pairs, chunk, width), BF16),
            pltpu.VMEM((pairs, right_width, right_width), BF16),
            pltpu.VMEM((all_pairs, all_pairs), BF16),
            pltpu.VMEM((all_pairs, all_pairs), BF16),
            pltpu.VMEM((all_pairs, chunk * width), BF16),
            pltpu.VMEM((all_pairs, chunk * width), BF16),
            pltpu.VMEM((chunks, all_pairs, chunk, width), BF16),
            pltpu.VMEM((chunks, n, pairs, chunk, width), BF16),
            pltpu.VMEM((sectors, roots, rows, right_width), BF16),
            pltpu.VMEM((n, roots, rows, right_width), BF16),
            pltpu.VMEM((roots, n * rows, right_width), BF16),
            pltpu.VMEM((pairs, width, roots * right_width), BF16),
            pltpu.VMEM((n * rows, block * width), BF16),
            pltpu.VMEM((n * rows, roots * right_width), F32),
            pltpu.VMEM((2, n // 2, chunks, chunk, roots * right_width), BF16),
            pltpu.VMEM((n // 2, chunks, chunk, roots * right_width), BF16),
            pltpu.VMEM((n // 2, chunks, chunk, roots * right_width), BF16),
            pltpu.VMEM((n // 2, chunks, chunk, roots * right_width), BF16),
            dma((2,)), dma, dma,
            dma((sectors,)), dma((sectors,)),
            dma((n,)), dma((n,)),
            dma((chunks, blocks, n)), dma((chunks, blocks, n)),
            dma((chunks, blocks, n)), dma((chunks, blocks, n)),
            dma, dma,
            dma((n // 2,)), dma((n // 2,)),
        ],
        compiler_params=pltpu.CompilerParams(
            collective_id=0, has_side_effects=True, vmem_limit_bytes=67043328
        ),
    )(left_ops, rotation, integrals, right_ops, states, sector_sizes, couplings,
      pair_order)
    return sigma[None]


def solution(mesh):
    placed = (
        P("sec", "pair", None, None),
        P("sec", None, None),
        P(),
        P("sec", "pair", None, None),
        P("sec", None, "pair", None),
        P("sec"),
        P("sec", None),
        P(),
    )
    return jax.shard_map(
        functools.partial(local, mesh.shape["pair"], mesh.shape["sec"]),
        mesh=mesh, in_specs=placed, out_specs=P("sec", None, "pair", None), check_vma=False,
    )
```
